32 devices in a mesh: grp: 2 (over y), epoch: 4 (over z), tile: 2 (over x), sub: 2 (over core).
Axes of the slice: x: 2, y: 2, z: 4, core: 2. Of those that a mesh axis runs over, the one named last changes fastest.
Arguments:
- epoch_images: float32 [32, 512, 512], P(('grp', 'epoch'), ('tile', 'sub')), parts along dimension 0, may hold values from -8 to 8
- psf_bank: float32 [16, 16, 16], replicated, may hold values from 0.05 to 1
- psf_index: int32 [32], P(('grp', 'epoch')), parts along dimension 0, may hold values from 0 to 15
- flux_scale: float32 [32], P(('grp', 'epoch')), parts along dimension 0, may hold values from 0.3 to 3
- noise_level: float32 [32], P(('grp', 'epoch')), parts along dimension 0, may hold values from 0.5 to 2
- src_row: int32 [8192], P('grp'), parts along dimension 0, may hold values from 0 to 511
- src_col: int32 [8192], P('grp'), parts along dimension 0, may hold values from 0 to 511
Outputs:
- difference: float32 [32, 512, 512], P(('grp', 'epoch'), ('tile', 'sub')), parts along dimension 0
- fluxes: float32 [32, 4096], P(('grp', 'epoch'), ('tile', 'sub')), parts along dimension 0
The draws below stay inside these ranges and needn't reach their ends.
There are 2 independent parts, one for each index of `grp`. The reference program is written for one: setup_inputs(seed, part) draws one part's arguments, and reference() takes and returns one part's arrays. A program takes and returns all parts, laid end to end along the dimension named above; an argument that names none is the same for every part. Nothing has to cross between parts.
All inputs are finite; a program needn't handle non-finite values.
Results may differ from the reference program's by a relative error of at most 0.0003.
Values sent between devices are 32-bit elements; how exact they have to be, the bound alone decides.
A program may use at most 128 MiB of HBM per device.

```python
import math
import jax
import jax.numpy as jnp
from jax import lax

TILE = 512
STAMP = 16
NPSF = 16
NSRC = 4096
EPOCHS = 16


def with_ends(entries, own_key, low, top_value):
    dims = entries.shape
    place = [jax.random.randint(jax.random.fold_in(own_key, axis), (), 0, dims[axis]) for axis in range(len(dims))]
    entries = entries.at[tuple(place)].set(low)
    longest = dims.index(max(dims))
    place[longest] = (place[longest] + 1) % dims[longest]
    return entries.at[tuple(place)].set(top_value)


def shard_levels(key, extent, shards, low, top_value):
    factor_of, own = 1.0, jax.random.fold_in(key, 6)
    for position, parts in shards:
        steps = jnp.exp(jax.random.uniform(jax.random.fold_in(own, position), (parts,), jnp.float32, low / len(shards), top_value / len(shards)))
        factor_of = factor_of * jnp.repeat(steps, extent[position] // parts).reshape([-1 if axis == position else 1 for axis in range(len(extent))])
    return factor_of


def bell_draw(stream_key, extent, scale, limit, split=(), kind=jnp.bfloat16):
    values = scale * jax.random.normal(stream_key, extent, jnp.float32)
    if split:
        values = values * shard_levels(stream_key, extent, split, -0.22, 0.18)
    return jnp.clip(values, -limit, limit).astype(kind)


def setup_inputs(seed: int = 0, part: int = 0) -> dict:
    splits = jax.random.split(jax.random.key(seed), 8)
    own_keys = jax.random.split(jax.random.fold_in(splits[7], part), 8)
    return {
        "epoch_images": bell_draw(own_keys[0], (EPOCHS, TILE, TILE), 1.0, 8.0, ((0, 4), (1, 4)), jnp.float32),
        "psf_bank": jnp.clip(jax.random.uniform(splits[1], (NPSF, STAMP, STAMP), jnp.float32, 0.05, 1.0), 0.05, 1.0),
        "psf_index": with_ends(jax.random.randint(own_keys[2], (EPOCHS,), 0, NPSF), jax.random.fold_in(own_keys[2], 1), 0, NPSF - 1).astype(jnp.int32),
        "flux_scale": jnp.clip(jnp.exp(math.log(3.0) - 2.3025851 * jax.random.uniform(own_keys[3], (EPOCHS,), jnp.float32) ** shard_levels(own_keys[3], (EPOCHS,), ((0, 4),), -0.2, 0.2)), 0.3, 3.0),
        "noise_level": jnp.clip(jnp.exp(math.log(2.0) - 1.3862944 * jax.random.uniform(own_keys[4], (EPOCHS,), jnp.float32) ** shard_levels(own_keys[4], (EPOCHS,), ((0, 4),), -0.2, 0.2)), 0.5, 2.0),
        "src_row": with_ends(jax.random.randint(own_keys[5], (NSRC,), 0, TILE), jax.random.fold_in(own_keys[5], 1), 0, TILE - 1).astype(jnp.int32),
        "src_col": with_ends(jax.random.randint(own_keys[6], (NSRC,), 0, TILE), jax.random.fold_in(own_keys[6], 1), 0, TILE - 1).astype(jnp.int32),
    }


def reference(epoch_images, psf_bank, psf_index, flux_scale, noise_level, src_row, src_col):
    stamps = psf_bank[psf_index]
    stamps = stamps / lax.optimization_barrier(jnp.sum(stamps, axis=(1, 2), keepdims=True))
    sumsq = lax.optimization_barrier(jnp.sum(stamps * stamps, axis=(1, 2)))
    padded = jnp.zeros((EPOCHS, TILE, TILE), stamps.dtype).at[:, :STAMP, :STAMP].set(stamps)
    padded = jnp.roll(padded, (-(STAMP // 2), -(STAMP // 2)), (1, 2))
    psf_hat = jnp.fft.fft2(padded)
    image_hat = jnp.fft.fft2(epoch_images)
    psf_power = jnp.real(psf_hat) ** 2 + jnp.imag(psf_hat) ** 2
    weight = (flux_scale / noise_level ** 2)[:, None, None]
    numer = lax.optimization_barrier(jnp.sum(weight * jnp.conj(psf_hat) * image_hat, axis=0))
    q_total = lax.optimization_barrier(jnp.sum((flux_scale ** 2 / noise_level ** 2)[:, None, None] * psf_power, axis=0)) + 0.01
    root_q = jnp.sqrt(q_total)
    template = numer / root_q
    scale = flux_scale[:, None, None]
    noise_norm = jnp.sqrt(noise_level[:, None, None] ** 2 * q_total + scale ** 2 * psf_power + 0.01)
    diff_hat = (root_q * image_hat - scale * psf_hat * template) / noise_norm
    difference = jnp.real(jnp.fft.ifft2(diff_hat))
    flux_map = jnp.real(jnp.fft.ifft2(diff_hat * jnp.conj(psf_hat))) / sumsq[:, None, None]
    fluxes = flux_map[:, src_row, src_col]
    return (difference, fluxes)
```

```python
import functools
import math

import jax
import jax.numpy as jnp
import numpy as np
from jax import lax
from jax.experimental import pallas as pl
from jax.experimental.pallas import tpu as pltpu
from jax.sharding import PartitionSpec as P

reg_floor = 0.01
MESH = pl.DeviceIdType.MESH
pad_rows = 8


def halves(table):
    table = jnp.asarray(table, jnp.float32)
    high = table.astype(jnp.bfloat16)
    return high, (table - high.astype(jnp.float32)).astype(jnp.bfloat16)


def trig(first, second, length):
    angle = (np.outer(first, second) % length) * (2.0 * math.pi / length)
    return np.cos(angle), np.sin(angle)


def numpy_halves(table):
    table = np.asarray(table, np.float32)
    high = table.astype(jnp.bfloat16)
    return high, (table - high.astype(np.float32)).astype(jnp.bfloat16)


def make_tables(side, slabs, stamp):
    block = side // (2 * slabs)
    whole = np.arange(side)
    rows = []
    stamp_cols = []
    offsets = np.arange(stamp) - stamp // 2
    for slab in range(slabs):
        freq = slab * block + np.arange(block)
        cosine, sine = trig(freq, whole, side)
        sine = -sine
        if slab == 0:
            sine[0] = np.where(whole % 2 == 0, 1.0, -1.0)
        rows += [cosine, sine]
        cosine, sine = trig(freq, offsets, side)
        extra_re = np.zeros((pad_rows, stamp))
        extra_im = np.zeros((pad_rows, stamp))
        if slab == 0:
            nyq_cos, nyq_sin = trig(np.array([side // 2]), offsets, side)
            extra_re[0] = nyq_cos[0]
            extra_im[0] = -nyq_sin[0]
        stamp_cols.append(np.concatenate([cosine, extra_re, -sine, extra_im]))
    row_hi, row_lo = numpy_halves(np.concatenate(rows))
    cosine, sine = trig(whole, whole, side)
    col_hi, col_lo = numpy_halves(np.concatenate([cosine, sine], axis=1))
    cosine, sine = trig(offsets, whole, side)
    hi, lo = numpy_halves(np.concatenate([cosine, sine], axis=1))
    stamp_rows = np.concatenate([hi, hi, lo])
    return row_hi, row_lo, col_hi, col_lo, np.stack(stamp_cols).astype(np.float32), stamp_rows


def split(value):
    high = value.astype(jnp.bfloat16)
    return high, (value - high.astype(jnp.float32)).astype(jnp.bfloat16)


def mul(left, right, contract=((1,), (0,))):
    return lax.dot_general(left, right, (contract, ((), ())), preferred_element_type=jnp.float32)


def kernel(
    slabs, subs, groups, img, bank, index, flux, noise, srow, scol,
    row_hi, row_lo, col_hi, col_lo, stamp_cols, stamp_rows,
    diff_out, flux_out,
    fwd_send, fwd_recv, bwd_send, bwd_recv, spec, filt_hi, filt_lo, psf, inv_sq, weight_own, weight_recv,
    quot, part, part_recv, block, full, pick_row, pick_tab, fl_send, fl_recv,
    s_fs, s_fr, s_bs, s_br, s_ws, s_wr, s_rs, s_rr, s_as, s_ar, s_xs, s_xr,
):
    f32 = jnp.float32
    epochs, slab_rows, side = img.shape
    stamps = bank.shape[0]
    half = side // (2 * slabs)
    ext = half + pad_rows
    width = side // groups
    per_dest = fl_send.shape[2]
    chunk = min(512, per_dest)
    chunks = per_dest // chunk
    tile = lax.axis_index("tile")
    sub = lax.axis_index("sub")
    me = tile * subs + sub
    zed = lax.axis_index("epoch")

    def slab_peer(step):
        other = lax.rem(me + step, slabs)
        return other, {"tile": other // subs, "sub": lax.rem(other, subs)}

    def zed_peer(step):
        other = lax.rem(zed + step, groups)
        return other, {"epoch": other}

    slab_order = sorted(range(1, slabs), key=lambda step: step % subs == 0, reverse=True)
    slab_order = [s for s in slab_order]

    barrier = pltpu.get_barrier_semaphore()
    for step in range(1, slabs):
        pl.semaphore_signal(barrier, inc=1, device_id=slab_peer(step)[1], device_id_type=MESH)
    for step in range(1, groups):
        pl.semaphore_signal(barrier, inc=1, device_id=zed_peer(step)[1], device_id_type=MESH)

    for e in range(epochs):
        hi, lo = split(img[e])
        nt = ((1,), (1,))
        fwd = mul(row_hi[...], hi, nt) + mul(row_hi[...], lo, nt) + mul(row_lo[...], hi, nt)
        fwd_send[e] = fwd.reshape(slabs, 2 * half, slab_rows)
        if e == 0:
            pl.semaphore_wait(barrier, slabs - 1 + groups - 1)
        for step in slab_order:
            other, where = slab_peer(step)
            pltpu.make_async_remote_copy(
                src_ref=fwd_send.at[e, other], dst_ref=fwd_recv.at[e, me],
                send_sem=s_fs.at[step, e], recv_sem=s_fr.at[step, e],
                device_id=where, device_id_type=MESH,
            ).start()
        fwd_recv[e, me] = fwd_send[e, me]

    lane = lax.broadcasted_iota(jnp.int32, (8, 128), 1)
    wsum = jnp.zeros((8, 128), f32)
    for e in range(epochs):
        ratio = jnp.full((8, 128), flux[e], f32) / jnp.full((8, 128), noise[e], f32)
        wsum = wsum + jnp.where(lane == index[e], ratio * ratio, 0.0)
    weight_own[...] = wsum
    for step in range(1, groups):
        _, where = zed_peer(step)
        pltpu.make_async_remote_copy(
            src_ref=weight_own, dst_ref=weight_recv.at[step],
            send_sem=s_ws.at[step], recv_sem=s_wr.at[step], device_id=where, device_id_type=MESH,
        ).start()

    cols = stamp_cols[me]
    group_lane = lax.broadcasted_iota(jnp.int32, (2 * ext, 3 * bank.shape[1]), 1)
    middle = (group_lane >= bank.shape[1]) & (group_lane < 2 * bank.shape[1])

    def stamp_body(k, carry):
        stamp = bank[k]
        total = jnp.sum(jnp.sum(stamp, axis=1, keepdims=True), axis=0, keepdims=True)
        stamp = stamp / total
        square = jnp.sum(jnp.sum(stamp * stamp, axis=1, keepdims=True), axis=0, keepdims=True)
        inv_sq[k] = jnp.broadcast_to(1.0 / square, (8, 128))
        wide = jnp.concatenate([stamp, stamp, stamp], axis=0)
        part_spec = lax.dot_general(
            cols, wide, (((1,), (1,)), ((), ())), precision=lax.Precision.HIGHEST, preferred_element_type=f32
        )
        high = part_spec.astype(jnp.bfloat16).astype(f32)
        left = jnp.where(middle, part_spec - high, high).astype(jnp.bfloat16)
        both = mul(left, stamp_rows[...])
        psf[k, 0] = both[:ext, :side] + both[ext:, side:]
        psf[k, 1] = both[ext:, :side] - both[:ext, side:]
        return carry

    lax.fori_loop(0, stamps, stamp_body, 0)

    for step in range(1, groups):
        _, where = zed_peer(step)
        pltpu.make_async_remote_copy(
            src_ref=weight_own, dst_ref=weight_recv.at[step],
            send_sem=s_ws.at[step], recv_sem=s_wr.at[step], device_id=where, device_id_type=MESH,
        ).wait()
        wsum = wsum + weight_recv[step]
    total_q = jnp.full((ext, side), reg_floor, f32)
    for k in range(stamps):
        re = psf[k, 0]
        im = psf[k, 1]
        total_q = total_q + wsum[0:1, k : k + 1] * (re * re + im * im)
    quot[0] = total_q
    quot[1] = jnp.sqrt(total_q)

    mine = pl.ds(pl.multiple_of(me * 2 * half, 2 * half), 2 * half)
    pixel = lax.broadcasted_iota(jnp.int32, (side, chunk), 0)

    def pick_body(c, carry):
        at = pl.ds(pl.multiple_of(c * chunk, chunk), chunk)
        pick_row[c] = jnp.where(pixel == srow[:, at], 1.0, 0.0).astype(jnp.bfloat16)
        hot = jnp.where(pixel == scol[:, at], 1.0, 0.0).astype(jnp.bfloat16)
        pick_tab[c] = mul(row_hi[mine, :], hot) + mul(row_lo[mine, :], hot)
        return carry

    lax.fori_loop(0, chunks * slabs, pick_body, 0)

    first = (lax.broadcasted_iota(jnp.int32, (half, side), 0) == 0) & (me == 0)
    first_ext = (lax.broadcasted_iota(jnp.int32, (pad_rows, side), 0) == 0) & (me == 0)
    zero_pad = jnp.zeros((pad_rows, side), f32)
    num_re = jnp.zeros((ext, side), f32)
    num_im = jnp.zeros((ext, side), f32)
    for e in range(epochs):
        for step in slab_order:
            other, where = slab_peer(step)
            pltpu.make_async_remote_copy(
                src_ref=fwd_send.at[e, other], dst_ref=fwd_recv.at[e, me],
                send_sem=s_fs.at[step, e], recv_sem=s_fr.at[step, e],
                device_id=where, device_id_type=MESH,
            ).wait()
        if slab_rows % 128 == 0:
            pieces = [(0, side, jnp.concatenate([fwd_recv[e, s] for s in range(slabs)], axis=1))]
        else:
            pieces = [(s * slab_rows, slab_rows, fwd_recv[e, s]) for s in range(slabs)]
        both = None
        for start, size, value in pieces:
            hi, lo = split(value)
            high_tab = col_hi[start : start + size, :]
            term = mul(hi, high_tab) + mul(lo, high_tab) + mul(hi, col_lo[start : start + size, :])
            both = term if both is None else both + term
        a_re, b_re = both[:half, :side], both[:half, side:]
        a_im, b_im = both[half:, :side], both[half:, side:]
        img_re = jnp.concatenate(
            [a_re + jnp.where(first, 0.0, b_im), jnp.where(first_ext, a_im[:pad_rows], zero_pad)], axis=0
        )
        img_im = jnp.concatenate(
            [jnp.where(first, 0.0, a_im) - b_re, jnp.where(first_ext, -b_im[:pad_rows], zero_pad)], axis=0
        )
        spec[e, 0] = img_re
        spec[e, 1] = img_im
        psf_re = psf[index[e], 0]
        psf_im = psf[index[e], 1]
        sig = jnp.full((1, side), noise[e], f32)
        weight = jnp.full((1, side), flux[e], f32) / (sig * sig)
        num_re = num_re + weight * (psf_re * img_re + psf_im * img_im)
        num_im = num_im + weight * (psf_re * img_im - psf_im * img_re)

    for g in range(groups):
        part[g, 0] = num_re[:, g * width : (g + 1) * width]
        part[g, 1] = num_im[:, g * width : (g + 1) * width]
    for step in range(1, groups):
        other, where = zed_peer(step)
        pltpu.make_async_remote_copy(
            src_ref=part.at[other], dst_ref=part_recv.at[step],
            send_sem=s_rs.at[step], recv_sem=s_rr.at[step], device_id=where, device_id_type=MESH,
        ).start()
    total = part[zed]
    for step in range(1, groups):
        other, where = zed_peer(step)
        pltpu.make_async_remote_copy(
            src_ref=part.at[other], dst_ref=part_recv.at[step],
            send_sem=s_rs.at[step], recv_sem=s_rr.at[step], device_id=where, device_id_type=MESH,
        ).wait()
        total = total + part_recv[step]
    block[...] = total
    for step in range(1, groups):
        other, where = zed_peer(step)
        pltpu.make_async_remote_copy(
            src_ref=block, dst_ref=full.at[zed],
            send_sem=s_as.at[step], recv_sem=s_ar.at[step], device_id=where, device_id_type=MESH,
        ).start()
    full[zed] = total
    for step in range(1, groups):
        other, where = zed_peer(step)
        pltpu.make_async_remote_copy(
            src_ref=block, dst_ref=full.at[zed],
            send_sem=s_as.at[step], recv_sem=s_ar.at[step], device_id=where, device_id_type=MESH,
        ).wait()
    root_q = quot[1]
    inv_root = 1.0 / root_q
    templ_re = jnp.concatenate([full[g, 0] for g in range(groups)], axis=1) * inv_root
    templ_im = jnp.concatenate([full[g, 1] for g in range(groups)], axis=1) * inv_root

    line = lax.broadcasted_iota(jnp.int32, (ext, side), 0)
    single = ((line == 0) & (me == 0)) | (line >= half)
    norm = jnp.where(single, 1.0 / (side * side), 2.0 / (side * side))

    def back(value_re, value_im):
        hi, lo = split(jnp.concatenate([value_re, value_im], axis=0))
        both = mul(hi, col_hi[...]) + mul(lo, col_hi[...]) + mul(hi, col_lo[...])
        g_re = both[:ext, :side] - both[ext:, side:]
        g_im = both[ext:, :side] + both[:ext, side:]
        nyq = g_re[half:, :]
        head = jnp.where(first_ext, nyq, g_im[:pad_rows])
        return jnp.concatenate([g_re[:half], head, g_im[pad_rows:half]], axis=0)

    for e in range(epochs):
        psf_re = psf[index[e], 0]
        psf_im = psf[index[e], 1]
        img_re = spec[e, 0]
        img_im = spec[e, 1]
        sig = jnp.full((1, side), noise[e], f32)
        scale = jnp.full((1, side), flux[e], f32)
        power = psf_re * psf_re + psf_im * psf_im
        inv = norm / jnp.sqrt(sig * sig * quot[0] + scale * scale * power + reg_floor)
        d_re = (root_q * img_re - scale * (psf_re * templ_re - psf_im * templ_im)) * inv
        d_im = (root_q * img_im - scale * (psf_re * templ_im + psf_im * templ_re)) * inv
        spec[e, 0] = d_re
        spec[e, 1] = d_im
        planes = back(d_re, d_im)
        for s in range(slabs):
            bwd_send[e, s] = planes[:, s * slab_rows : (s + 1) * slab_rows]
        for step in slab_order:
            other, where = slab_peer(step)
            pltpu.make_async_remote_copy(
                src_ref=bwd_send.at[e, other], dst_ref=bwd_recv.at[e, me],
                send_sem=s_bs.at[step, e], recv_sem=s_br.at[step, e],
                device_id=where, device_id_type=MESH,
            ).start()
        bwd_recv[e, me] = bwd_send[e, me]

    for e in range(epochs):
        psf_re = psf[index[e], 0]
        psf_im = psf[index[e], 1]
        d_re = spec[e, 0]
        d_im = spec[e, 1]
        inv = inv_sq[index[e]][0:1, 0:1]
        hi, lo = split(back((d_re * psf_re + d_im * psf_im) * inv, (d_im * psf_re - d_re * psf_im) * inv))
        filt_hi[e * 2 * half : (e + 1) * 2 * half, :] = hi
        filt_lo[e * 2 * half : (e + 1) * 2 * half, :] = lo

    def flux_body(c, carry):
        got = mul(filt_hi[...], pick_row[c]) + mul(filt_lo[...], pick_row[c])
        got = got.reshape(epochs, 2 * half, chunk) * pick_tab[c][None]
        fl_send[c // chunks, :, pl.ds(pl.multiple_of(lax.rem(c, chunks) * chunk, chunk), chunk)] = jnp.sum(got, axis=1)
        return carry

    lax.fori_loop(0, chunks * slabs, flux_body, 0)
    for step in slab_order:
        other, where = slab_peer(step)
        pltpu.make_async_remote_copy(
            src_ref=fl_send.at[other], dst_ref=fl_recv.at[step],
            send_sem=s_xs.at[step], recv_sem=s_xr.at[step], device_id=where, device_id_type=MESH,
        ).start()

    for e in range(epochs):
        for step in slab_order:
            other, where = slab_peer(step)
            pltpu.make_async_remote_copy(
                src_ref=bwd_send.at[e, other], dst_ref=bwd_recv.at[e, me],
                send_sem=s_bs.at[step, e], recv_sem=s_br.at[step, e],
                device_id=where, device_id_type=MESH,
            ).wait()
        hi, lo = split(bwd_recv[e].reshape(side, slab_rows))
        tn = ((0,), (0,))
        diff_out[e] = mul(hi, row_hi[...], tn) + mul(lo, row_hi[...], tn) + mul(hi, row_lo[...], tn)

    total = fl_send[me]
    for step in slab_order:
        other, where = slab_peer(step)
        pltpu.make_async_remote_copy(
            src_ref=fl_send.at[other], dst_ref=fl_recv.at[step],
            send_sem=s_xs.at[step], recv_sem=s_xr.at[step], device_id=where, device_id_type=MESH,
        ).wait()
        total = total + fl_recv[step]
    flux_out[...] = total


def shards(slabs, subs, groups, tables, images, bank, index, flux, noise, src_row, src_col):
    epochs, slab_rows, side = images.shape
    stamps, stamp, _ = bank.shape
    sources = src_row.shape[0]
    half = side // (2 * slabs)
    ext = half + pad_rows
    width = side // groups
    per_dest = sources // slabs
    chunk = min(512, per_dest)
    f32 = jnp.float32
    vmem = pl.BlockSpec(memory_space=pltpu.VMEM)
    smem = pl.BlockSpec(memory_space=pltpu.SMEM)
    dma = pltpu.SemaphoreType.DMA
    plane = pltpu.VMEM((epochs, slabs, 2 * half, slab_rows), f32)
    return pl.pallas_call(
        functools.partial(kernel, slabs, subs, groups),
        out_shape=(
            jax.ShapeDtypeStruct((epochs, slab_rows, side), f32),
            jax.ShapeDtypeStruct((epochs, per_dest), f32),
        ),
        in_specs=[vmem, vmem, smem, smem, smem] + [vmem] * 8,
        out_specs=(vmem, vmem),
        scratch_shapes=[
            plane, plane, plane, plane,
            pltpu.VMEM((epochs, 2, ext, side), f32),
            pltpu.VMEM((epochs * 2 * half, side), jnp.bfloat16),
            pltpu.VMEM((epochs * 2 * half, side), jnp.bfloat16),
            pltpu.VMEM((stamps, 2, ext, side), f32),
            pltpu.VMEM((stamps, 8, 128), f32),
            pltpu.VMEM((8, 128), f32),
            pltpu.VMEM((groups, 8, 128), f32),
            pltpu.VMEM((2, ext, side), f32),
            pltpu.VMEM((groups, 2, ext, width), f32),
            pltpu.VMEM((groups, 2, ext, width), f32),
            pltpu.VMEM((2, ext, width), f32),
            pltpu.VMEM((groups, 2, ext, width), f32),
            pltpu.VMEM((sources // chunk, side, chunk), jnp.bfloat16),
            pltpu.VMEM((sources // chunk, 2 * half, chunk), f32),
            pltpu.VMEM((slabs, epochs, per_dest), f32),
            pltpu.VMEM((slabs, epochs, per_dest), f32),
            dma((slabs, epochs)), dma((slabs, epochs)), dma((slabs, epochs)), dma((slabs, epochs)),
            dma((groups,)), dma((groups,)), dma((groups,)), dma((groups,)), dma((groups,)), dma((groups,)),
            dma((slabs,)), dma((slabs,)),
        ],
        compiler_params=pltpu.CompilerParams(
            collective_id=0, has_side_effects=True, vmem_limit_bytes=60 * 1024 * 1024
        ),
        name="zogy",
    )(images, bank, index, flux, noise, src_row.reshape(1, sources), src_col.reshape(1, sources), *tables)


def solution(mesh):
    subs = mesh.shape["sub"]
    slabs = mesh.shape["tile"] * subs
    groups = mesh.shape["epoch"]
    in_specs = (
        P(("grp", "epoch"), ("tile", "sub"), None),
        P(),
        P(("grp", "epoch")),
        P(("grp", "epoch")),
        P(("grp", "epoch")),
        P("grp"),
        P("grp"),
    )
    out_specs = (P(("grp", "epoch"), ("tile", "sub"), None), P(("grp", "epoch"), ("tile", "sub")))

    def run(images, bank, index, flux, noise, src_row, src_col):
        tables = make_tables(images.shape[2], slabs, bank.shape[1])
        body = functools.partial(shards, slabs, subs, groups, tables)
        return jax.shard_map(body, mesh=mesh, in_specs=in_specs, out_specs=out_specs, check_vma=False)(
            images, bank, index, flux, noise, src_row, src_col
        )

    return run
```

```python
import functools
import math

import jax
import jax.numpy as jnp
import numpy as np
from jax import lax
from jax.experimental import pallas as pl
from jax.experimental.pallas import tpu as pltpu
from jax.sharding import PartitionSpec as P

reg_floor = 0.01
MESH = pl.DeviceIdType.MESH
pad_rows = 8


def halves(table):
    table = jnp.asarray(table, jnp.float32)
    high = table.astype(jnp.bfloat16)
    return high, (table - high.astype(jnp.float32)).astype(jnp.bfloat16)


def trig(first, second, length):
    angle = (np.outer(first, second) % length) * (2.0 * math.pi / length)
    return np.cos(angle), np.sin(angle)


def numpy_halves(table):
    table = np.asarray(table, np.float32)
    high = table.astype(jnp.bfloat16)
    return high, (table - high.astype(np.float32)).astype(jnp.bfloat16)


def make_tables(side, slabs, stamp):
    block = side // (2 * slabs)
    whole = np.arange(side)
    rows = []
    stamp_cols = []
    offsets = np.arange(stamp) - stamp // 2
    for slab in range(slabs):
        freq = slab * block + np.arange(block)
        cosine, sine = trig(freq, whole, side)
        sine = -sine
        if slab == 0:
            sine[0] = np.where(whole % 2 == 0, 1.0, -1.0)
        rows += [cosine, sine]
        cosine, sine = trig(freq, offsets, side)
        extra_re = np.zeros((pad_rows, stamp))
        extra_im = np.zeros((pad_rows, stamp))
        if slab == 0:
            nyq_cos, nyq_sin = trig(np.array([side // 2]), offsets, side)
            extra_re[0] = nyq_cos[0]
            extra_im[0] = -nyq_sin[0]
        stamp_cols.append(np.concatenate([cosine, extra_re, -sine, extra_im]))
    row_hi, row_lo = numpy_halves(np.concatenate(rows))
    cosine, sine = trig(whole, whole, side)
    col_hi, col_lo = numpy_halves(np.concatenate([cosine, sine], axis=1))
    cosine, sine = trig(offsets, whole, side)
    hi, lo = numpy_halves(np.concatenate([cosine, sine], axis=1))
    stamp_rows = np.concatenate([hi, hi, lo])
    return row_hi, row_lo, col_hi, col_lo, np.stack(stamp_cols).astype(np.float32), stamp_rows


def split(value):
    high = value.astype(jnp.bfloat16)
    return high, (value - high.astype(jnp.float32)).astype(jnp.bfloat16)


def mul(left, right, contract=((1,), (0,))):
    return lax.dot_general(left, right, (contract, ((), ())), preferred_element_type=jnp.float32)


def kernel(
    slabs, subs, groups, img, bank, index, flux, noise, srow, scol,
    row_hi, row_lo, col_hi, col_lo, stamp_cols, stamp_rows,
    diff_out, flux_out,
    fwd_send, fwd_recv, bwd_send, bwd_recv, spec, filt_hi, filt_lo, psf, inv_sq, weight_own, weight_recv,
    quot, part, part_recv, block, full, pick_row, pick_tab, fl_send, fl_recv,
    s_fs, s_fr, s_bs, s_br, s_ws, s_wr, s_rs, s_rr, s_as, s_ar, s_xs, s_xr,
):
    f32 = jnp.float32
    epochs, slab_rows, side = img.shape
    stamps = bank.shape[0]
    half = side // (2 * slabs)
    ext = half + pad_rows
    width = side // groups
    per_dest = fl_send.shape[2]
    chunk = min(512, per_dest)
    chunks = per_dest // chunk
    tile = lax.axis_index("tile")
    sub = lax.axis_index("sub")
    me = tile * subs + sub
    zed = lax.axis_index("epoch")

    def slab_peer(step):
        other = lax.rem(me + step, slabs)
        return other, {"tile": other // subs, "sub": lax.rem(other, subs)}

    def zed_peer(step):
        other = lax.rem(zed + step, groups)
        return other, {"epoch": other}

    slab_order = sorted(range(1, slabs), key=lambda step: step % subs == 0, reverse=True)
    slab_order = [s for s in slab_order]

    barrier = pltpu.get_barrier_semaphore()
    for step in range(1, slabs):
        pl.semaphore_signal(barrier, inc=1, device_id=slab_peer(step)[1], device_id_type=MESH)
    for step in range(1, groups):
        pl.semaphore_signal(barrier, inc=1, device_id=zed_peer(step)[1], device_id_type=MESH)

    for e in range(epochs):
        hi, lo = split(img[e])
        nt = ((1,), (1,))
        fwd = mul(row_hi[...], hi, nt) + mul(row_hi[...], lo, nt) + mul(row_lo[...], hi, nt)
        fwd_send[e] = fwd.reshape(slabs, 2 * half, slab_rows)
        if e == 0:
            pl.semaphore_wait(barrier, slabs - 1 + groups - 1)
        for step in slab_order:
            other, where = slab_peer(step)
            pltpu.make_async_remote_copy(
                src_ref=fwd_send.at[e, other], dst_ref=fwd_recv.at[e, me],
                send_sem=s_fs.at[step, e], recv_sem=s_fr.at[step, e],
                device_id=where, device_id_type=MESH,
            ).start()
        fwd_recv[e, me] = fwd_send[e, me]

    lane = lax.broadcasted_iota(jnp.int32, (8, 128), 1)
    wsum = jnp.zeros((8, 128), f32)
    for e in range(epochs):
        ratio = jnp.full((8, 128), flux[e], f32) / jnp.full((8, 128), noise[e], f32)
        wsum = wsum + jnp.where(lane == index[e], ratio * ratio, 0.0)
    weight_own[...] = wsum
    for step in range(1, groups):
        _, where = zed_peer(step)
        pltpu.make_async_remote_copy(
            src_ref=weight_own, dst_ref=weight_recv.at[step],
            send_sem=s_ws.at[step], recv_sem=s_wr.at[step], device_id=where, device_id_type=MESH,
        ).start()

    cols = stamp_cols[me]
    batch = 4 if stamps % 4 == 0 else 1
    group_lane = lax.broadcasted_iota(jnp.int32, (batch * 2 * ext, 3 * bank.shape[1]), 1)
    middle = (group_lane >= bank.shape[1]) & (group_lane < 2 * bank.shape[1])

    def stamp_body(group, carry):
        parts = []
        for i in range(batch):
            k = group * batch + i
            stamp = bank[k]
            total = jnp.sum(jnp.sum(stamp, axis=1, keepdims=True), axis=0, keepdims=True)
            stamp = stamp / total
            square = jnp.sum(jnp.sum(stamp * stamp, axis=1, keepdims=True), axis=0, keepdims=True)
            inv_sq[k] = jnp.broadcast_to(1.0 / square, (8, 128))
            wide = jnp.concatenate([stamp, stamp, stamp], axis=0)
            parts.append(
                lax.dot_general(
                    cols, wide, (((1,), (1,)), ((), ())),
                    precision=lax.Precision.HIGHEST, preferred_element_type=f32,
                )
            )
        part_spec = jnp.concatenate(parts, axis=0)
        high = part_spec.astype(jnp.bfloat16).astype(f32)
        left = jnp.where(middle, part_spec - high, high).astype(jnp.bfloat16)
        every = mul(left, stamp_rows[...])
        for i in range(batch):
            both = every[i * 2 * ext : (i + 1) * 2 * ext]
            psf[group * batch + i, 0] = both[:ext, :side] + both[ext:, side:]
            psf[group * batch + i, 1] = both[ext:, :side] - both[:ext, side:]
        return carry

    lax.fori_loop(0, stamps // batch, stamp_body, 0)

    for step in range(1, groups):
        _, where = zed_peer(step)
        pltpu.make_async_remote_copy(
            src_ref=weight_own, dst_ref=weight_recv.at[step],
            send_sem=s_ws.at[step], recv_sem=s_wr.at[step], device_id=where, device_id_type=MESH,
        ).wait()
        wsum = wsum + weight_recv[step]
    total_q = jnp.full((ext, side), reg_floor, f32)
    for k in range(stamps):
        re = psf[k, 0]
        im = psf[k, 1]
        total_q = total_q + wsum[0:1, k : k + 1] * (re * re + im * im)
    quot[0] = total_q
    quot[1] = jnp.sqrt(total_q)

    mine = pl.ds(pl.multiple_of(me * 2 * half, 2 * half), 2 * half)
    pixel = lax.broadcasted_iota(jnp.int32, (side, chunk), 0)

    def pick_body(c, carry):
        at = pl.ds(pl.multiple_of(c * chunk, chunk), chunk)
        pick_row[c] = jnp.where(pixel == srow[:, at], 1.0, 0.0).astype(jnp.bfloat16)
        hot = jnp.where(pixel == scol[:, at], 1.0, 0.0).astype(jnp.bfloat16)
        pick_tab[c] = mul(row_hi[mine, :], hot) + mul(row_lo[mine, :], hot)
        return carry

    picks = chunks * slabs

    first = (lax.broadcasted_iota(jnp.int32, (half, side), 0) == 0) & (me == 0)
    first_ext = (lax.broadcasted_iota(jnp.int32, (pad_rows, side), 0) == 0) & (me == 0)
    zero_pad = jnp.zeros((pad_rows, side), f32)
    num_re = jnp.zeros((ext, side), f32)
    num_im = jnp.zeros((ext, side), f32)
    for e in range(epochs):
        for step in slab_order:
            other, where = slab_peer(step)
            pltpu.make_async_remote_copy(
                src_ref=fwd_send.at[e, other], dst_ref=fwd_recv.at[e, me],
                send_sem=s_fs.at[step, e], recv_sem=s_fr.at[step, e],
                device_id=where, device_id_type=MESH,
            ).wait()
        if slab_rows % 128 == 0:
            pieces = [(0, side, jnp.concatenate([fwd_recv[e, s] for s in range(slabs)], axis=1))]
        else:
            pieces = [(s * slab_rows, slab_rows, fwd_recv[e, s]) for s in range(slabs)]
        both = None
        for start, size, value in pieces:
            hi, lo = split(value)
            high_tab = col_hi[start : start + size, :]
            term = mul(hi, high_tab) + mul(lo, high_tab) + mul(hi, col_lo[start : start + size, :])
            both = term if both is None else both + term
        a_re, b_re = both[:half, :side], both[:half, side:]
        a_im, b_im = both[half:, :side], both[half:, side:]
        img_re = jnp.concatenate(
            [a_re + jnp.where(first, 0.0, b_im), jnp.where(first_ext, a_im[:pad_rows], zero_pad)], axis=0
        )
        img_im = jnp.concatenate(
            [jnp.where(first, 0.0, a_im) - b_re, jnp.where(first_ext, -b_im[:pad_rows], zero_pad)], axis=0
        )
        spec[e, 0] = img_re
        spec[e, 1] = img_im
        psf_re = psf[index[e], 0]
        psf_im = psf[index[e], 1]
        sig = jnp.full((1, side), noise[e], f32)
        weight = jnp.full((1, side), flux[e], f32) / (sig * sig)
        num_re = num_re + weight * (psf_re * img_re + psf_im * img_im)
        num_im = num_im + weight * (psf_re * img_im - psf_im * img_re)

    for g in range(groups):
        part[g, 0] = num_re[:, g * width : (g + 1) * width]
        part[g, 1] = num_im[:, g * width : (g + 1) * width]
    for step in range(1, groups):
        other, where = zed_peer(step)
        pltpu.make_async_remote_copy(
            src_ref=part.at[other], dst_ref=part_recv.at[step],
            send_sem=s_rs.at[step], recv_sem=s_rr.at[step], device_id=where, device_id_type=MESH,
        ).start()
    lax.fori_loop(0, picks // 2, pick_body, 0)
    total = part[zed]
    for step in range(1, groups):
        other, where = zed_peer(step)
        pltpu.make_async_remote_copy(
            src_ref=part.at[other], dst_ref=part_recv.at[step],
            send_sem=s_rs.at[step], recv_sem=s_rr.at[step], device_id=where, device_id_type=MESH,
        ).wait()
        total = total + part_recv[step]
    block[...] = total
    for step in range(1, groups):
        other, where = zed_peer(step)
        pltpu.make_async_remote_copy(
            src_ref=block, dst_ref=full.at[zed],
            send_sem=s_as.at[step], recv_sem=s_ar.at[step], device_id=where, device_id_type=MESH,
        ).start()
    full[zed] = total
    lax.fori_loop(picks // 2, picks, pick_body, 0)
    for step in range(1, groups):
        other, where = zed_peer(step)
        pltpu.make_async_remote_copy(
            src_ref=block, dst_ref=full.at[zed],
            send_sem=s_as.at[step], recv_sem=s_ar.at[step], device_id=where, device_id_type=MESH,
        ).wait()
    root_q = quot[1]
    inv_root = 1.0 / root_q
    templ_re = jnp.concatenate([full[g, 0] for g in range(groups)], axis=1) * inv_root
    templ_im = jnp.concatenate([full[g, 1] for g in range(groups)], axis=1) * inv_root

    line = lax.broadcasted_iota(jnp.int32, (ext, side), 0)
    single = ((line == 0) & (me == 0)) | (line >= half)
    norm = jnp.where(single, 1.0 / (side * side), 2.0 / (side * side))

    def back(value_re, value_im):
        hi, lo = split(jnp.concatenate([value_re, value_im], axis=0))
        both = mul(hi, col_hi[...]) + mul(lo, col_hi[...]) + mul(hi, col_lo[...])
        g_re = both[:ext, :side] - both[ext:, side:]
        g_im = both[ext:, :side] + both[:ext, side:]
        nyq = g_re[half:, :]
        head = jnp.where(first_ext, nyq, g_im[:pad_rows])
        return jnp.concatenate([g_re[:half], head, g_im[pad_rows:half]], axis=0)

    for e in range(epochs):
        psf_re = psf[index[e], 0]
        psf_im = psf[index[e], 1]
        img_re = spec[e, 0]
        img_im = spec[e, 1]
        sig = jnp.full((1, side), noise[e], f32)
        scale = jnp.full((1, side), flux[e], f32)
        power = psf_re * psf_re + psf_im * psf_im
        inv = norm / jnp.sqrt(sig * sig * quot[0] + scale * scale * power + reg_floor)
        d_re = (root_q * img_re - scale * (psf_re * templ_re - psf_im * templ_im)) * inv
        d_im = (root_q * img_im - scale * (psf_re * templ_im + psf_im * templ_re)) * inv
        spec[e, 0] = d_re
        spec[e, 1] = d_im
        planes = back(d_re, d_im)
        for s in range(slabs):
            bwd_send[e, s] = planes[:, s * slab_rows : (s + 1) * slab_rows]
        for step in slab_order:
            other, where = slab_peer(step)
            pltpu.make_async_remote_copy(
                src_ref=bwd_send.at[e, other], dst_ref=bwd_recv.at[e, me],
                send_sem=s_bs.at[step, e], recv_sem=s_br.at[step, e],
                device_id=where, device_id_type=MESH,
            ).start()
        bwd_recv[e, me] = bwd_send[e, me]

    for e in range(epochs):
        psf_re = psf[index[e], 0]
        psf_im = psf[index[e], 1]
        d_re = spec[e, 0]
        d_im = spec[e, 1]
        inv = inv_sq[index[e]][0:1, 0:1]
        hi, lo = split(back((d_re * psf_re + d_im * psf_im) * inv, (d_im * psf_re - d_re * psf_im) * inv))
        filt_hi[e * 2 * half : (e + 1) * 2 * half, :] = hi
        filt_lo[e * 2 * half : (e + 1) * 2 * half, :] = lo

    def flux_body(c, carry):
        got = mul(filt_hi[...], pick_row[c]) + mul(filt_lo[...], pick_row[c])
        got = got.reshape(epochs, 2 * half, chunk) * pick_tab[c][None]
        fl_send[c // chunks, :, pl.ds(pl.multiple_of(lax.rem(c, chunks) * chunk, chunk), chunk)] = jnp.sum(got, axis=1)
        return carry

    lax.fori_loop(0, chunks * slabs, flux_body, 0)
    for step in slab_order:
        other, where = slab_peer(step)
        pltpu.make_async_remote_copy(
            src_ref=fl_send.at[other], dst_ref=fl_recv.at[step],
            send_sem=s_xs.at[step], recv_sem=s_xr.at[step], device_id=where, device_id_type=MESH,
        ).start()

    for e in range(epochs):
        for step in slab_order:
            other, where = slab_peer(step)
            pltpu.make_async_remote_copy(
                src_ref=bwd_send.at[e, other], dst_ref=bwd_recv.at[e, me],
                send_sem=s_bs.at[step, e], recv_sem=s_br.at[step, e],
                device_id=where, device_id_type=MESH,
            ).wait()
        hi, lo = split(bwd_recv[e].reshape(side, slab_rows))
        tn = ((0,), (0,))
        diff_out[e] = mul(hi, row_hi[...], tn) + mul(lo, row_hi[...], tn) + mul(hi, row_lo[...], tn)

    total = fl_send[me]
    for step in slab_order:
        other, where = slab_peer(step)
        pltpu.make_async_remote_copy(
            src_ref=fl_send.at[other], dst_ref=fl_recv.at[step],
            send_sem=s_xs.at[step], recv_sem=s_xr.at[step], device_id=where, device_id_type=MESH,
        ).wait()
        total = total + fl_recv[step]
    flux_out[...] = total


def shards(slabs, subs, groups, tables, images, bank, index, flux, noise, src_row, src_col):
    epochs, slab_rows, side = images.shape
    stamps, stamp, _ = bank.shape
    sources = src_row.shape[0]
    half = side // (2 * slabs)
    ext = half + pad_rows
    width = side // groups
    per_dest = sources // slabs
    chunk = min(512, per_dest)
    f32 = jnp.float32
    vmem = pl.BlockSpec(memory_space=pltpu.VMEM)
    smem = pl.BlockSpec(memory_space=pltpu.SMEM)
    dma = pltpu.SemaphoreType.DMA
    plane = pltpu.VMEM((epochs, slabs, 2 * half, slab_rows), f32)
    return pl.pallas_call(
        functools.partial(kernel, slabs, subs, groups),
        out_shape=(
            jax.ShapeDtypeStruct((epochs, slab_rows, side), f32),
            jax.ShapeDtypeStruct((epochs, per_dest), f32),
        ),
        in_specs=[vmem, vmem, smem, smem, smem] + [vmem] * 8,
        out_specs=(vmem, vmem),
        scratch_shapes=[
            plane, plane, plane, plane,
            pltpu.VMEM((epochs, 2, ext, side), f32),
            pltpu.VMEM((epochs * 2 * half, side), jnp.bfloat16),
            pltpu.VMEM((epochs * 2 * half, side), jnp.bfloat16),
            pltpu.VMEM((stamps, 2, ext, side), f32),
            pltpu.VMEM((stamps, 8, 128), f32),
            pltpu.VMEM((8, 128), f32),
            pltpu.VMEM((groups, 8, 128), f32),
            pltpu.VMEM((2, ext, side), f32),
            pltpu.VMEM((groups, 2, ext, width), f32),
            pltpu.VMEM((groups, 2, ext, width), f32),
            pltpu.VMEM((2, ext, width), f32),
            pltpu.VMEM((groups, 2, ext, width), f32),
            pltpu.VMEM((sources // chunk, side, chunk), jnp.bfloat16),
            pltpu.VMEM((sources // chunk, 2 * half, chunk), f32),
            pltpu.VMEM((slabs, epochs, per_dest), f32),
            pltpu.VMEM((slabs, epochs, per_dest), f32),
            dma((slabs, epochs)), dma((slabs, epochs)), dma((slabs, epochs)), dma((slabs, epochs)),
            dma((groups,)), dma((groups,)), dma((groups,)), dma((groups,)), dma((groups,)), dma((groups,)),
            dma((slabs,)), dma((slabs,)),
        ],
        compiler_params=pltpu.CompilerParams(
            collective_id=0, has_side_effects=True, vmem_limit_bytes=60 * 1024 * 1024
        ),
        name="zogy",
    )(images, bank, index, flux, noise, src_row.reshape(1, sources), src_col.reshape(1, sources), *tables)


def solution(mesh):
    subs = mesh.shape["sub"]
    slabs = mesh.shape["tile"] * subs
    groups = mesh.shape["epoch"]
    in_specs = (
        P(("grp", "epoch"), ("tile", "sub"), None),
        P(),
        P(("grp", "epoch")),
        P(("grp", "epoch")),
        P(("grp", "epoch")),
        P("grp"),
        P("grp"),
    )
    out_specs = (P(("grp", "epoch"), ("tile", "sub"), None), P(("grp", "epoch"), ("tile", "sub")))

    def run(images, bank, index, flux, noise, src_row, src_col):
        tables = make_tables(images.shape[2], slabs, bank.shape[1])
        body = functools.partial(shards, slabs, subs, groups, tables)
        return jax.shard_map(body, mesh=mesh, in_specs=in_specs, out_specs=out_specs, check_vma=False)(
            images, bank, index, flux, noise, src_row, src_col
        )

    return run
```

```python
import functools
import math

import jax
import jax.numpy as jnp
import numpy as np
from jax import lax
from jax.experimental import pallas as pl
from jax.experimental.pallas import tpu as pltpu
from jax.sharding import PartitionSpec as P

reg_floor = 0.01
MESH = pl.DeviceIdType.MESH
pad_rows = 8
strips = 2


def trig(first, second, length):
    angle = (np.outer(first, second) % length) * (2.0 * math.pi / length)
    return np.cos(angle), np.sin(angle)


def numpy_halves(table):
    table = np.asarray(table, np.float32)
    high = table.astype(jnp.bfloat16)
    return high, (table - high.astype(np.float32)).astype(jnp.bfloat16)


def make_tables(side, slabs, stamp):
    strip = side // (2 * slabs * strips)
    whole = np.arange(side)
    offsets = np.arange(stamp) - stamp // 2
    rows = [[] for _ in range(strips)]
    stamp_cols = []
    for slab in range(slabs):
        own = []
        for h in range(strips):
            freq = (slab * strips + h) * strip + np.arange(strip)
            cosine, sine = trig(freq, whole, side)
            sine = -sine
            if slab == 0 and h == 0:
                sine[0] = np.where(whole % 2 == 0, 1.0, -1.0)
            rows[h] += [cosine, sine]
            cosine, sine = trig(freq, offsets, side)
            extra = np.zeros((2, pad_rows if h == 0 else 0, stamp))
            if slab == 0 and h == 0:
                nyq_cos, nyq_sin = trig(np.array([side // 2]), offsets, side)
                extra[0, 0] = nyq_cos[0]
                extra[1, 0] = -nyq_sin[0]
            own += [cosine, extra[0], -sine, extra[1]]
        stamp_cols.append(np.concatenate(own))
    row_hi, row_lo = numpy_halves(np.stack([np.concatenate(part) for part in rows]))
    cosine, sine = trig(whole, whole, side)
    col_hi, col_lo = numpy_halves(np.concatenate([cosine, sine], axis=1))
    cosine, sine = trig(offsets, whole, side)
    hi, lo = numpy_halves(np.concatenate([cosine, sine], axis=1))
    stamp_rows = np.concatenate([hi, hi, lo])
    return row_hi, row_lo, col_hi, col_lo, np.stack(stamp_cols).astype(np.float32), stamp_rows


def split(value):
    high = value.astype(jnp.bfloat16)
    return high, (value - high.astype(jnp.float32)).astype(jnp.bfloat16)


def mul(left, right, contract=((1,), (0,))):
    return lax.dot_general(left, right, (contract, ((), ())), preferred_element_type=jnp.float32)


def kernel(
    slabs, subs, groups, img, bank, index, flux, noise, srow, scol,
    row_hi, row_lo, col_hi, col_lo, stamp_cols, stamp_rows,
    diff_out, flux_out,
    fwd_send, fwd_recv, bwd_send, bwd_recv, spec, filt_hi, filt_lo, psf, inv_sq, weight_own, weight_recv,
    quot, part, part_recv, block, full, pick_row, pick_tab, fl_send, fl_recv,
    s_fs, s_fr, s_bs, s_br, s_ws, s_wr, s_rs, s_rr, s_as, s_ar, s_xs, s_xr,
):
    f32 = jnp.float32
    epochs, slab_rows, side = img.shape
    stamps = bank.shape[0]
    half = side // (2 * slabs)
    strip = half // strips
    pair = 2 * strip
    exts = [strip + pad_rows] + [strip] * (strips - 1)
    width = side // groups
    per_dest = fl_send.shape[2]
    chunk = min(512, per_dest)
    chunks = per_dest // chunk
    tile = lax.axis_index("tile")
    sub = lax.axis_index("sub")
    me = tile * subs + sub
    zed = lax.axis_index("epoch")

    def slab_peer(step):
        other = lax.rem(me + step, slabs)
        return other, {"tile": other // subs, "sub": lax.rem(other, subs)}

    def zed_peer(step):
        other = lax.rem(zed + step, groups)
        return other, {"epoch": other}

    slab_order = sorted(range(1, slabs), key=lambda step: step % subs == 0, reverse=True)
    slab_order = [s for s in slab_order]

    barrier = pltpu.get_barrier_semaphore()
    for step in range(1, slabs):
        pl.semaphore_signal(barrier, inc=1, device_id=slab_peer(step)[1], device_id_type=MESH)
    for step in range(1, groups):
        pl.semaphore_signal(barrier, inc=1, device_id=zed_peer(step)[1], device_id_type=MESH)

    def slab_copy(send, recv, ssem, rsem, h, step):
        other, where = slab_peer(step)
        return pltpu.make_async_remote_copy(
            src_ref=send.at[h, other], dst_ref=recv.at[h, me],
            send_sem=ssem.at[step, h], recv_sem=rsem.at[step, h],
            device_id=where, device_id_type=MESH,
        )

    pixels = img[...].reshape(epochs * slab_rows, side)
    hi, lo = split(pixels)
    nt = ((1,), (1,))
    for h in range(strips):
        fwd = mul(row_hi[h], hi, nt) + mul(row_hi[h], lo, nt) + mul(row_lo[h], hi, nt)
        for s in range(slabs):
            for e in range(epochs):
                fwd_send[h, s, e] = fwd[s * pair : (s + 1) * pair, e * slab_rows : (e + 1) * slab_rows]
        if h == 0:
            pl.semaphore_wait(barrier, slabs - 1 + groups - 1)
        for step in slab_order:
            slab_copy(fwd_send, fwd_recv, s_fs, s_fr, h, step).start()
        fwd_recv[h, me] = fwd_send[h, me]

    lane = lax.broadcasted_iota(jnp.int32, (8, 128), 1)
    wsum = jnp.zeros((8, 128), f32)
    for e in range(epochs):
        ratio = jnp.full((8, 128), flux[e], f32) / jnp.full((8, 128), noise[e], f32)
        wsum = wsum + jnp.where(lane == index[e], ratio * ratio, 0.0)
    weight_own[...] = wsum
    for step in range(1, groups):
        _, where = zed_peer(step)
        pltpu.make_async_remote_copy(
            src_ref=weight_own, dst_ref=weight_recv.at[step],
            send_sem=s_ws.at[step], recv_sem=s_wr.at[step], device_id=where, device_id_type=MESH,
        ).start()

    cols = stamp_cols[me]
    batch = 4 if stamps % 4 == 0 else 1
    group_lane = lax.broadcasted_iota(jnp.int32, (batch * cols.shape[0], 3 * bank.shape[1]), 1)
    middle = (group_lane >= bank.shape[1]) & (group_lane < 2 * bank.shape[1])

    def stamp_body(group, carry):
        parts = []
        for i in range(batch):
            k = group * batch + i
            stamp = bank[k]
            total = jnp.sum(jnp.sum(stamp, axis=1, keepdims=True), axis=0, keepdims=True)
            stamp = stamp / total
            square = jnp.sum(jnp.sum(stamp * stamp, axis=1, keepdims=True), axis=0, keepdims=True)
            inv_sq[k] = jnp.broadcast_to(1.0 / square, (8, 128))
            wide = jnp.concatenate([stamp, stamp, stamp], axis=0)
            parts.append(
                lax.dot_general(
                    cols, wide, (((1,), (1,)), ((), ())),
                    precision=lax.Precision.HIGHEST, preferred_element_type=f32,
                )
            )
        part_spec = jnp.concatenate(parts, axis=0)
        high = part_spec.astype(jnp.bfloat16).astype(f32)
        left = jnp.where(middle, part_spec - high, high).astype(jnp.bfloat16)
        every = mul(left, stamp_rows[...])
        for i in range(batch):
            base = i * cols.shape[0]
            for h, ext in enumerate(exts):
                re, im = every[base : base + ext], every[base + ext : base + 2 * ext]
                base += 2 * ext
                psf[h, group * batch + i, 0, :ext] = re[:, :side] + im[:, side:]
                psf[h, group * batch + i, 1, :ext] = im[:, :side] - re[:, side:]
        return carry

    lax.fori_loop(0, stamps // batch, stamp_body, 0)

    for step in range(1, groups):
        _, where = zed_peer(step)
        pltpu.make_async_remote_copy(
            src_ref=weight_own, dst_ref=weight_recv.at[step],
            send_sem=s_ws.at[step], recv_sem=s_wr.at[step], device_id=where, device_id_type=MESH,
        ).wait()
        wsum = wsum + weight_recv[step]
    for h, ext in enumerate(exts):
        total_q = jnp.full((ext, side), reg_floor, f32)
        for k in range(stamps):
            re = psf[h, k, 0, :ext]
            im = psf[h, k, 1, :ext]
            total_q = total_q + wsum[0:1, k : k + 1] * (re * re + im * im)
        quot[h, 0, :ext] = total_q
        quot[h, 1, :ext] = jnp.sqrt(total_q)

    mine = pl.ds(pl.multiple_of(me * pair, pair), pair)
    pixel = lax.broadcasted_iota(jnp.int32, (side, chunk), 0)

    def pick_body(c, carry):
        at = pl.ds(pl.multiple_of(c * chunk, chunk), chunk)
        pick_row[c] = jnp.where(pixel == srow[:, at], 1.0, 0.0).astype(jnp.bfloat16)
        hot = jnp.where(pixel == scol[:, at], 1.0, 0.0).astype(jnp.bfloat16)
        for h in range(strips):
            pick_tab[c, h * pair : (h + 1) * pair] = mul(row_hi[h, mine, :], hot) + mul(row_lo[h, mine, :], hot)
        return carry

    picks = chunks * slabs

    first = (lax.broadcasted_iota(jnp.int32, (strip, side), 0) == 0) & (me == 0)
    first_ext = (lax.broadcasted_iota(jnp.int32, (pad_rows, side), 0) == 0) & (me == 0)

    def reduce_copy(h, step):
        other, where = zed_peer(step)
        rows = pl.ds(0, exts[h])
        return pltpu.make_async_remote_copy(
            src_ref=part.at[h, other, :, rows], dst_ref=part_recv.at[h, step, :, rows],
            send_sem=s_rs.at[step, h], recv_sem=s_rr.at[step, h], device_id=where, device_id_type=MESH,
        )

    def gather_copy(h, step):
        other, where = zed_peer(step)
        rows = pl.ds(0, exts[h])
        return pltpu.make_async_remote_copy(
            src_ref=block.at[h, :, rows], dst_ref=full.at[h, zed, :, rows],
            send_sem=s_as.at[step, h], recv_sem=s_ar.at[step, h], device_id=where, device_id_type=MESH,
        )

    def forward(h):
        ext = exts[h]
        for step in slab_order:
            slab_copy(fwd_send, fwd_recv, s_fs, s_fr, h, step).wait()
        lines = [fwd_recv[h, s].reshape(epochs * pair, slab_rows) for s in range(slabs)]
        if slab_rows % 128 == 0:
            pieces = [(0, side, jnp.concatenate(lines, axis=1))]
        else:
            pieces = [(s * slab_rows, slab_rows, lines[s]) for s in range(slabs)]
        every = None
        for start, size, value in pieces:
            hi, lo = split(value)
            high_tab = col_hi[start : start + size, :]
            term = mul(hi, high_tab) + mul(lo, high_tab) + mul(hi, col_lo[start : start + size, :])
            every = term if every is None else every + term
        num_re = jnp.zeros((ext, side), f32)
        num_im = jnp.zeros((ext, side), f32)
        for e in range(epochs):
            both = every[e * pair : (e + 1) * pair]
            a_re, b_re = both[:strip, :side], both[:strip, side:]
            a_im, b_im = both[strip:, :side], both[strip:, side:]
            if h == 0:
                img_re = jnp.concatenate(
                    [a_re + jnp.where(first, 0.0, b_im), jnp.where(first_ext, a_im[:pad_rows], 0.0)], axis=0
                )
                img_im = jnp.concatenate(
                    [jnp.where(first, 0.0, a_im) - b_re, jnp.where(first_ext, -b_im[:pad_rows], 0.0)], axis=0
                )
            else:
                img_re = a_re + b_im
                img_im = a_im - b_re
            spec[h, e, 0, :ext] = img_re
            spec[h, e, 1, :ext] = img_im
            psf_re = psf[h, index[e], 0, :ext]
            psf_im = psf[h, index[e], 1, :ext]
            sig = jnp.full((1, side), noise[e], f32)
            weight = jnp.full((1, side), flux[e], f32) / (sig * sig)
            num_re = num_re + weight * (psf_re * img_re + psf_im * img_im)
            num_im = num_im + weight * (psf_re * img_im - psf_im * img_re)
        for g in range(groups):
            part[h, g, 0, :ext] = num_re[:, g * width : (g + 1) * width]
            part[h, g, 1, :ext] = num_im[:, g * width : (g + 1) * width]
        for step in range(1, groups):
            reduce_copy(h, step).start()

    def reduce(h):
        ext = exts[h]
        total = part[h, zed, :, :ext]
        for step in range(1, groups):
            reduce_copy(h, step).wait()
            total = total + part_recv[h, step, :, :ext]
        block[h, :, :ext] = total
        for step in range(1, groups):
            gather_copy(h, step).start()
        full[h, zed, :, :ext] = total

    def back(h, planes_re, planes_im):
        ext = exts[h]
        hi, lo = split(jnp.concatenate([x for re_im in zip(planes_re, planes_im) for x in re_im], axis=0))
        every = mul(hi, col_hi[...]) + mul(lo, col_hi[...]) + mul(hi, col_lo[...])
        out = []
        for e in range(epochs):
            both = every[e * 2 * ext : (e + 1) * 2 * ext]
            g_re = both[:ext, :side] - both[ext:, side:]
            g_im = both[ext:, :side] + both[:ext, side:]
            if h == 0:
                head = jnp.where(first_ext, g_re[strip:], g_im[:pad_rows])
                out.append(jnp.concatenate([g_re[:strip], head, g_im[pad_rows:strip]], axis=0))
            else:
                out.append(jnp.concatenate([g_re, g_im], axis=0))
        return out

    def differences(h):
        ext = exts[h]
        for step in range(1, groups):
            gather_copy(h, step).wait()
        root_q = quot[h, 1, :ext]
        inv_root = 1.0 / root_q
        templ_re = jnp.concatenate([full[h, g, 0, :ext] for g in range(groups)], axis=1) * inv_root
        templ_im = jnp.concatenate([full[h, g, 1, :ext] for g in range(groups)], axis=1) * inv_root
        norm = jnp.full((ext, side), 2.0 / (side * side), f32)
        if h == 0:
            line = lax.broadcasted_iota(jnp.int32, (ext, side), 0)
            norm = jnp.where(((line == 0) & (me == 0)) | (line >= strip), 1.0 / (side * side), norm)
        planes_re, planes_im = [], []
        for e in range(epochs):
            psf_re = psf[h, index[e], 0, :ext]
            psf_im = psf[h, index[e], 1, :ext]
            img_re = spec[h, e, 0, :ext]
            img_im = spec[h, e, 1, :ext]
            sig = jnp.full((1, side), noise[e], f32)
            scale = jnp.full((1, side), flux[e], f32)
            power = psf_re * psf_re + psf_im * psf_im
            inv = norm / jnp.sqrt(sig * sig * quot[h, 0, :ext] + scale * scale * power + reg_floor)
            d_re = (root_q * img_re - scale * (psf_re * templ_re - psf_im * templ_im)) * inv
            d_im = (root_q * img_im - scale * (psf_re * templ_im + psf_im * templ_re)) * inv
            spec[h, e, 0, :ext] = d_re
            spec[h, e, 1, :ext] = d_im
            planes_re.append(d_re)
            planes_im.append(d_im)
        for e, plane in enumerate(back(h, planes_re, planes_im)):
            for s in range(slabs):
                bwd_send[h, s, e] = plane[:, s * slab_rows : (s + 1) * slab_rows]
        for step in slab_order:
            slab_copy(bwd_send, bwd_recv, s_bs, s_br, h, step).start()
        bwd_recv[h, me] = bwd_send[h, me]

    def filtered(h):
        ext = exts[h]
        planes_re, planes_im = [], []
        for e in range(epochs):
            psf_re = psf[h, index[e], 0, :ext]
            psf_im = psf[h, index[e], 1, :ext]
            d_re = spec[h, e, 0, :ext]
            d_im = spec[h, e, 1, :ext]
            inv = inv_sq[index[e]][0:1, 0:1]
            planes_re.append((d_re * psf_re + d_im * psf_im) * inv)
            planes_im.append((d_im * psf_re - d_re * psf_im) * inv)
        for e, plane in enumerate(back(h, planes_re, planes_im)):
            hi, lo = split(plane)
            at = (e * strips + h) * pair
            filt_hi[at : at + pair, :] = hi
            filt_lo[at : at + pair, :] = lo

    def final(h):
        for step in slab_order:
            slab_copy(bwd_send, bwd_recv, s_bs, s_br, h, step).wait()
        tn = ((0,), (0,))
        for e in range(epochs):
            hi, lo = split(bwd_recv[h, :, e].reshape(slabs * pair, slab_rows))
            out = mul(hi, row_hi[h], tn) + mul(lo, row_hi[h], tn) + mul(hi, row_lo[h], tn)
            diff_out[e] = out if h == 0 else diff_out[e] + out

    picks = chunks * slabs
    forward(0)
    lax.fori_loop(0, picks // 2, pick_body, 0)
    for h in range(1, strips):
        forward(h)
        reduce(h - 1)
    lax.fori_loop(picks // 2, picks, pick_body, 0)
    reduce(strips - 1)
    for h in range(strips):
        differences(h)
        filtered(h)

    def flux_body(c, carry):
        got = mul(filt_hi[...], pick_row[c]) + mul(filt_lo[...], pick_row[c])
        got = got.reshape(epochs, 2 * half, chunk) * pick_tab[c][None]
        fl_send[c // chunks, :, pl.ds(pl.multiple_of(lax.rem(c, chunks) * chunk, chunk), chunk)] = jnp.sum(got, axis=1)
        return carry

    lax.fori_loop(0, chunks * slabs, flux_body, 0)
    for step in slab_order:
        other, where = slab_peer(step)
        pltpu.make_async_remote_copy(
            src_ref=fl_send.at[other], dst_ref=fl_recv.at[step],
            send_sem=s_xs.at[step], recv_sem=s_xr.at[step], device_id=where, device_id_type=MESH,
        ).start()

    for h in range(strips):
        final(h)

    total = fl_send[me]
    for step in slab_order:
        other, where = slab_peer(step)
        pltpu.make_async_remote_copy(
            src_ref=fl_send.at[other], dst_ref=fl_recv.at[step],
            send_sem=s_xs.at[step], recv_sem=s_xr.at[step], device_id=where, device_id_type=MESH,
        ).wait()
        total = total + fl_recv[step]
    flux_out[...] = total


def shards(slabs, subs, groups, tables, images, bank, index, flux, noise, src_row, src_col):
    epochs, slab_rows, side = images.shape
    stamps, stamp, _ = bank.shape
    sources = src_row.shape[0]
    half = side // (2 * slabs)
    ext = half // strips + pad_rows
    width = side // groups
    per_dest = sources // slabs
    chunk = min(512, per_dest)
    f32 = jnp.float32
    vmem = pl.BlockSpec(memory_space=pltpu.VMEM)
    smem = pl.BlockSpec(memory_space=pltpu.SMEM)
    dma = pltpu.SemaphoreType.DMA
    plane = pltpu.VMEM((strips, slabs, epochs, 2 * half // strips, slab_rows), f32)
    return pl.pallas_call(
        functools.partial(kernel, slabs, subs, groups),
        out_shape=(
            jax.ShapeDtypeStruct((epochs, slab_rows, side), f32),
            jax.ShapeDtypeStruct((epochs, per_dest), f32),
        ),
        in_specs=[vmem, vmem, smem, smem, smem] + [vmem] * 8,
        out_specs=(vmem, vmem),
        scratch_shapes=[
            plane, plane, plane, plane,
            pltpu.VMEM((strips, epochs, 2, ext, side), f32),
            pltpu.VMEM((epochs * 2 * half, side), jnp.bfloat16),
            pltpu.VMEM((epochs * 2 * half, side), jnp.bfloat16),
            pltpu.VMEM((strips, stamps, 2, ext, side), f32),
            pltpu.VMEM((stamps, 8, 128), f32),
            pltpu.VMEM((8, 128), f32),
            pltpu.VMEM((groups, 8, 128), f32),
            pltpu.VMEM((strips, 2, ext, side), f32),
            pltpu.VMEM((strips, groups, 2, ext, width), f32),
            pltpu.VMEM((strips, groups, 2, ext, width), f32),
            pltpu.VMEM((strips, 2, ext, width), f32),
            pltpu.VMEM((strips, groups, 2, ext, width), f32),
            pltpu.VMEM((sources // chunk, side, chunk), jnp.bfloat16),
            pltpu.VMEM((sources // chunk, 2 * half, chunk), f32),
            pltpu.VMEM((slabs, epochs, per_dest), f32),
            pltpu.VMEM((slabs, epochs, per_dest), f32),
            dma((slabs, strips)), dma((slabs, strips)), dma((slabs, strips)), dma((slabs, strips)),
            dma((groups,)), dma((groups,)),
            dma((groups, strips)), dma((groups, strips)), dma((groups, strips)), dma((groups, strips)),
            dma((slabs,)), dma((slabs,)),
        ],
        compiler_params=pltpu.CompilerParams(
            collective_id=0, has_side_effects=True, vmem_limit_bytes=60 * 1024 * 1024
        ),
        name="zogy",
    )(images, bank, index, flux, noise, src_row.reshape(1, sources), src_col.reshape(1, sources), *tables)


def solution(mesh):
    subs = mesh.shape["sub"]
    slabs = mesh.shape["tile"] * subs
    groups = mesh.shape["epoch"]
    in_specs = (
        P(("grp", "epoch"), ("tile", "sub"), None),
        P(),
        P(("grp", "epoch")),
        P(("grp", "epoch")),
        P(("grp", "epoch")),
        P("grp"),
        P("grp"),
    )
    out_specs = (P(("grp", "epoch"), ("tile", "sub"), None), P(("grp", "epoch"), ("tile", "sub")))

    def run(images, bank, index, flux, noise, src_row, src_col):
        tables = make_tables(images.shape[2], slabs, bank.shape[1])
        body = functools.partial(shards, slabs, subs, groups, tables)
        return jax.shard_map(body, mesh=mesh, in_specs=in_specs, out_specs=out_specs, check_vma=False)(
            images, bank, index, flux, noise, src_row, src_col
        )

    return run
```

```python
import functools
import math

import jax
import jax.numpy as jnp
import numpy as np
from jax import lax
from jax.experimental import pallas as pl
from jax.experimental.pallas import tpu as pltpu
from jax.sharding import PartitionSpec as P

reg_floor = 0.01
MESH = pl.DeviceIdType.MESH
pad_rows = 8
strips = 2


def trig(first, second, length):
    angle = (np.outer(first, second) % length) * (2.0 * math.pi / length)
    return np.cos(angle), np.sin(angle)


def numpy_halves(table):
    table = np.asarray(table, np.float32)
    high = table.astype(jnp.bfloat16)
    return high, (table - high.astype(np.float32)).astype(jnp.bfloat16)


def make_tables(side, slabs, stamp):
    strip = side // (2 * slabs * strips)
    whole = np.arange(side)
    offsets = np.arange(stamp) - stamp // 2
    rows = [[] for _ in range(strips)]
    stamp_cols = []
    for slab in range(slabs):
        own = []
        for h in range(strips):
            freq = (slab * strips + h) * strip + np.arange(strip)
            cosine, sine = trig(freq, whole, side)
            sine = -sine
            if slab == 0 and h == 0:
                sine[0] = np.where(whole % 2 == 0, 1.0, -1.0)
            rows[h] += [cosine, sine]
            cosine, sine = trig(freq, offsets, side)
            extra = np.zeros((2, pad_rows if h == 0 else 0, stamp))
            if slab == 0 and h == 0:
                nyq_cos, nyq_sin = trig(np.array([side // 2]), offsets, side)
                extra[0, 0] = nyq_cos[0]
                extra[1, 0] = -nyq_sin[0]
            own += [cosine, extra[0], -sine, extra[1]]
        stamp_cols.append(np.concatenate(own))
    row_hi, row_lo = numpy_halves(np.stack([np.concatenate(part) for part in rows]))
    cosine, sine = trig(whole, whole, side)
    col_hi, col_lo = numpy_halves(np.concatenate([cosine, sine], axis=1))
    cosine, sine = trig(offsets, whole, side)
    hi, lo = numpy_halves(np.concatenate([cosine, sine], axis=1))
    stamp_rows = np.concatenate([hi, hi, lo])
    return row_hi, row_lo, col_hi, col_lo, np.stack(stamp_cols).astype(np.float32), stamp_rows


def split(value):
    high = value.astype(jnp.bfloat16)
    return high, (value - high.astype(jnp.float32)).astype(jnp.bfloat16)


def mul(left, right, contract=((1,), (0,))):
    return lax.dot_general(left, right, (contract, ((), ())), preferred_element_type=jnp.float32)


def kernel(
    slabs, subs, groups, img, bank, index, flux, noise, srow, scol,
    row_hi, row_lo, col_hi, col_lo, stamp_cols, stamp_rows,
    diff_out, flux_out,
    fwd_send, fwd_recv, bwd_send, bwd_recv, spec, filt_hi, filt_lo, psf, inv_sq, weight_own, weight_recv,
    quot, part, part_recv, block, full, pick_row, pick_tab, fl_send, fl_recv,
    s_fs, s_fr, s_bs, s_br, s_ws, s_wr, s_rs, s_rr, s_as, s_ar, s_xs, s_xr,
):
    f32 = jnp.float32
    epochs, slab_rows, side = img.shape
    stamps = bank.shape[0]
    half = side // (2 * slabs)
    strip = half // strips
    pair = 2 * strip
    exts = [strip + pad_rows] + [strip] * (strips - 1)
    width = side // groups
    per_dest = fl_send.shape[2]
    chunk = min(512, per_dest)
    chunks = per_dest // chunk
    tile = lax.axis_index("tile")
    sub = lax.axis_index("sub")
    me = tile * subs + sub
    zed = lax.axis_index("epoch")

    def slab_peer(step):
        other = lax.rem(me + step, slabs)
        return other, {"tile": other // subs, "sub": lax.rem(other, subs)}

    def zed_peer(step):
        other = lax.rem(zed + step, groups)
        return other, {"epoch": other}

    slab_order = sorted(range(1, slabs), key=lambda step: step % subs == 0, reverse=True)
    slab_order = [s for s in slab_order]

    barrier = pltpu.get_barrier_semaphore()
    for step in range(1, slabs):
        pl.semaphore_signal(barrier, inc=1, device_id=slab_peer(step)[1], device_id_type=MESH)
    for step in range(1, groups):
        pl.semaphore_signal(barrier, inc=1, device_id=zed_peer(step)[1], device_id_type=MESH)

    def slab_copy(send, recv, ssem, rsem, h, step):
        other, where = slab_peer(step)
        return pltpu.make_async_remote_copy(
            src_ref=send.at[h, other], dst_ref=recv.at[h, me],
            send_sem=ssem.at[step, h], recv_sem=rsem.at[step, h],
            device_id=where, device_id_type=MESH,
        )

    pixels = img[...].reshape(epochs * slab_rows, side)
    hi, lo = split(pixels)
    nt = ((1,), (1,))
    for h in range(strips):
        fwd = mul(row_hi[h], hi, nt) + mul(row_hi[h], lo, nt) + mul(row_lo[h], hi, nt)
        for s in range(slabs):
            for e in range(epochs):
                fwd_send[h, s, e] = fwd[s * pair : (s + 1) * pair, e * slab_rows : (e + 1) * slab_rows]
        if h == 0:
            pl.semaphore_wait(barrier, slabs - 1 + groups - 1)
        for step in slab_order:
            slab_copy(fwd_send, fwd_recv, s_fs, s_fr, h, step).start()
        fwd_recv[h, me] = fwd_send[h, me]

    lane = lax.broadcasted_iota(jnp.int32, (8, 128), 1)
    wsum = jnp.zeros((8, 128), f32)
    for e in range(epochs):
        ratio = jnp.full((8, 128), flux[e], f32) / jnp.full((8, 128), noise[e], f32)
        wsum = wsum + jnp.where(lane == index[e], ratio * ratio, 0.0)
    weight_own[...] = wsum
    for step in range(1, groups):
        _, where = zed_peer(step)
        pltpu.make_async_remote_copy(
            src_ref=weight_own, dst_ref=weight_recv.at[step],
            send_sem=s_ws.at[step], recv_sem=s_wr.at[step], device_id=where, device_id_type=MESH,
        ).start()

    cols = stamp_cols[me]
    batch = 4 if stamps % 4 == 0 else 1
    group_lane = lax.broadcasted_iota(jnp.int32, (batch * cols.shape[0], 3 * bank.shape[1]), 1)
    middle = (group_lane >= bank.shape[1]) & (group_lane < 2 * bank.shape[1])

    def stamp_body(group, carry):
        parts = []
        for i in range(batch):
            k = group * batch + i
            stamp = bank[k]
            total = jnp.sum(jnp.sum(stamp, axis=1, keepdims=True), axis=0, keepdims=True)
            stamp = stamp / total
            square = jnp.sum(jnp.sum(stamp * stamp, axis=1, keepdims=True), axis=0, keepdims=True)
            inv_sq[k] = jnp.broadcast_to(1.0 / square, (8, 128))
            wide = jnp.concatenate([stamp, stamp, stamp], axis=0)
            parts.append(
                lax.dot_general(
                    cols, wide, (((1,), (1,)), ((), ())),
                    precision=lax.Precision.HIGHEST, preferred_element_type=f32,
                )
            )
        part_spec = jnp.concatenate(parts, axis=0)
        high = part_spec.astype(jnp.bfloat16).astype(f32)
        left = jnp.where(middle, part_spec - high, high).astype(jnp.bfloat16)
        every = mul(left, stamp_rows[...])
        for i in range(batch):
            base = i * cols.shape[0]
            for h, ext in enumerate(exts):
                re, im = every[base : base + ext], every[base + ext : base + 2 * ext]
                base += 2 * ext
                psf[h, group * batch + i, 0, :ext] = re[:, :side] + im[:, side:]
                psf[h, group * batch + i, 1, :ext] = im[:, :side] - re[:, side:]
        return carry

    lax.fori_loop(0, stamps // batch, stamp_body, 0)

    for step in range(1, groups):
        _, where = zed_peer(step)
        pltpu.make_async_remote_copy(
            src_ref=weight_own, dst_ref=weight_recv.at[step],
            send_sem=s_ws.at[step], recv_sem=s_wr.at[step], device_id=where, device_id_type=MESH,
        ).wait()
        wsum = wsum + weight_recv[step]
    for h, ext in enumerate(exts):
        total_q = jnp.full((ext, side), reg_floor, f32)
        for k in range(stamps):
            re = psf[h, k, 0, :ext]
            im = psf[h, k, 1, :ext]
            total_q = total_q + wsum[0:1, k : k + 1] * (re * re + im * im)
        quot[h, 0, :ext] = total_q
        quot[h, 1, :ext] = jnp.sqrt(total_q)

    mine = pl.ds(pl.multiple_of(me * pair, pair), pair)
    pixel = lax.broadcasted_iota(jnp.int32, (side, chunk), 0)

    def pick_body(c, carry):
        at = pl.ds(pl.multiple_of(c * chunk, chunk), chunk)
        pick_row[c] = jnp.where(pixel == srow[:, at], 1.0, 0.0).astype(jnp.bfloat16)
        hot = jnp.where(pixel == scol[:, at], 1.0, 0.0).astype(jnp.bfloat16)
        tables = [row_hi[h, mine, :] for h in range(strips)] + [row_lo[h, mine, :] for h in range(strips)]
        got = mul(jnp.concatenate(tables, axis=0), hot)
        pick_tab[c] = got[: 2 * half] + got[2 * half :]
        return carry

    picks = chunks * slabs

    first = (lax.broadcasted_iota(jnp.int32, (strip, side), 0) == 0) & (me == 0)
    first_ext = (lax.broadcasted_iota(jnp.int32, (pad_rows, side), 0) == 0) & (me == 0)

    def reduce_copy(h, step):
        other, where = zed_peer(step)
        rows = pl.ds(0, exts[h])
        return pltpu.make_async_remote_copy(
            src_ref=part.at[h, other, :, rows], dst_ref=part_recv.at[h, step, :, rows],
            send_sem=s_rs.at[step, h], recv_sem=s_rr.at[step, h], device_id=where, device_id_type=MESH,
        )

    def gather_copy(h, step):
        other, where = zed_peer(step)
        rows = pl.ds(0, exts[h])
        return pltpu.make_async_remote_copy(
            src_ref=block.at[h, :, rows], dst_ref=full.at[h, zed, :, rows],
            send_sem=s_as.at[step, h], recv_sem=s_ar.at[step, h], device_id=where, device_id_type=MESH,
        )

    def forward(h):
        ext = exts[h]
        for step in slab_order:
            slab_copy(fwd_send, fwd_recv, s_fs, s_fr, h, step).wait()
        lines = [fwd_recv[h, s].reshape(epochs * pair, slab_rows) for s in range(slabs)]
        if slab_rows % 128 == 0:
            pieces = [(0, side, jnp.concatenate(lines, axis=1))]
        else:
            pieces = [(s * slab_rows, slab_rows, lines[s]) for s in range(slabs)]
        every = None
        for start, size, value in pieces:
            hi, lo = split(value)
            high_tab = col_hi[start : start + size, :]
            term = mul(hi, high_tab) + mul(lo, high_tab) + mul(hi, col_lo[start : start + size, :])
            every = term if every is None else every + term
        num_re = jnp.zeros((ext, side), f32)
        num_im = jnp.zeros((ext, side), f32)
        for e in range(epochs):
            both = every[e * pair : (e + 1) * pair]
            a_re, b_re = both[:strip, :side], both[:strip, side:]
            a_im, b_im = both[strip:, :side], both[strip:, side:]
            if h == 0:
                img_re = jnp.concatenate(
                    [a_re + jnp.where(first, 0.0, b_im), jnp.where(first_ext, a_im[:pad_rows], 0.0)], axis=0
                )
                img_im = jnp.concatenate(
                    [jnp.where(first, 0.0, a_im) - b_re, jnp.where(first_ext, -b_im[:pad_rows], 0.0)], axis=0
                )
            else:
                img_re = a_re + b_im
                img_im = a_im - b_re
            spec[h, e, 0, :ext] = img_re
            spec[h, e, 1, :ext] = img_im
            psf_re = psf[h, index[e], 0, :ext]
            psf_im = psf[h, index[e], 1, :ext]
            sig = jnp.full((1, side), noise[e], f32)
            weight = jnp.full((1, side), flux[e], f32) / (sig * sig)
            num_re = num_re + weight * (psf_re * img_re + psf_im * img_im)
            num_im = num_im + weight * (psf_re * img_im - psf_im * img_re)
        for g in range(groups):
            part[h, g, 0, :ext] = num_re[:, g * width : (g + 1) * width]
            part[h, g, 1, :ext] = num_im[:, g * width : (g + 1) * width]
        for step in range(1, groups):
            reduce_copy(h, step).start()

    def reduce(h):
        ext = exts[h]
        total = part[h, zed, :, :ext]
        for step in range(1, groups):
            reduce_copy(h, step).wait()
            total = total + part_recv[h, step, :, :ext]
        block[h, :, :ext] = total
        for step in range(1, groups):
            gather_copy(h, step).start()
        full[h, zed, :, :ext] = total

    def back(h, planes_re, planes_im):
        ext = exts[h]
        hi, lo = split(jnp.concatenate([x for re_im in zip(planes_re, planes_im) for x in re_im], axis=0))
        every = mul(hi, col_hi[...]) + mul(lo, col_hi[...]) + mul(hi, col_lo[...])
        out = []
        for e in range(epochs):
            both = every[e * 2 * ext : (e + 1) * 2 * ext]
            g_re = both[:ext, :side] - both[ext:, side:]
            g_im = both[ext:, :side] + both[:ext, side:]
            if h == 0:
                head = jnp.where(first_ext, g_re[strip:], g_im[:pad_rows])
                out.append(jnp.concatenate([g_re[:strip], head, g_im[pad_rows:strip]], axis=0))
            else:
                out.append(jnp.concatenate([g_re, g_im], axis=0))
        return out

    def differences(h):
        ext = exts[h]
        for step in range(1, groups):
            gather_copy(h, step).wait()
        root_q = quot[h, 1, :ext]
        inv_root = 1.0 / root_q
        templ_re = jnp.concatenate([full[h, g, 0, :ext] for g in range(groups)], axis=1) * inv_root
        templ_im = jnp.concatenate([full[h, g, 1, :ext] for g in range(groups)], axis=1) * inv_root
        norm = jnp.full((ext, side), 2.0 / (side * side), f32)
        if h == 0:
            line = lax.broadcasted_iota(jnp.int32, (ext, side), 0)
            norm = jnp.where(((line == 0) & (me == 0)) | (line >= strip), 1.0 / (side * side), norm)
        planes_re, planes_im = [], []
        for e in range(epochs):
            psf_re = psf[h, index[e], 0, :ext]
            psf_im = psf[h, index[e], 1, :ext]
            img_re = spec[h, e, 0, :ext]
            img_im = spec[h, e, 1, :ext]
            sig = jnp.full((1, side), noise[e], f32)
            scale = jnp.full((1, side), flux[e], f32)
            power = psf_re * psf_re + psf_im * psf_im
            inv = norm / jnp.sqrt(sig * sig * quot[h, 0, :ext] + scale * scale * power + reg_floor)
            d_re = (root_q * img_re - scale * (psf_re * templ_re - psf_im * templ_im)) * inv
            d_im = (root_q * img_im - scale * (psf_re * templ_im + psf_im * templ_re)) * inv
            spec[h, e, 0, :ext] = d_re
            spec[h, e, 1, :ext] = d_im
            planes_re.append(d_re)
            planes_im.append(d_im)
        for e, plane in enumerate(back(h, planes_re, planes_im)):
            for s in range(slabs):
                bwd_send[h, s, e] = plane[:, s * slab_rows : (s + 1) * slab_rows]
        for step in slab_order:
            slab_copy(bwd_send, bwd_recv, s_bs, s_br, h, step).start()
        bwd_recv[h, me] = bwd_send[h, me]

    def filtered(h):
        ext = exts[h]
        planes_re, planes_im = [], []
        for e in range(epochs):
            psf_re = psf[h, index[e], 0, :ext]
            psf_im = psf[h, index[e], 1, :ext]
            d_re = spec[h, e, 0, :ext]
            d_im = spec[h, e, 1, :ext]
            inv = inv_sq[index[e]][0:1, 0:1]
            planes_re.append((d_re * psf_re + d_im * psf_im) * inv)
            planes_im.append((d_im * psf_re - d_re * psf_im) * inv)
        for e, plane in enumerate(back(h, planes_re, planes_im)):
            hi, lo = split(plane)
            at = (e * strips + h) * pair
            filt_hi[at : at + pair, :] = hi
            filt_lo[at : at + pair, :] = lo

    def final(h):
        for step in slab_order:
            slab_copy(bwd_send, bwd_recv, s_bs, s_br, h, step).wait()
        tn = ((0,), (0,))
        for e in range(epochs):
            hi, lo = split(bwd_recv[h, :, e].reshape(slabs * pair, slab_rows))
            out = mul(hi, row_hi[h], tn) + mul(lo, row_hi[h], tn) + mul(hi, row_lo[h], tn)
            diff_out[e] = out if h == 0 else diff_out[e] + out

    picks = chunks * slabs
    forward(0)
    lax.fori_loop(0, picks // 2, pick_body, 0)
    for h in range(1, strips):
        forward(h)
        reduce(h - 1)
    lax.fori_loop(picks // 2, picks, pick_body, 0)
    reduce(strips - 1)
    for h in range(strips):
        differences(h)
        filtered(h)

    def flux_body(c, carry):
        got = mul(filt_hi[...], pick_row[c]) + mul(filt_lo[...], pick_row[c])
        got = got.reshape(epochs, 2 * half, chunk) * pick_tab[c][None]
        fl_send[c // chunks, :, pl.ds(pl.multiple_of(lax.rem(c, chunks) * chunk, chunk), chunk)] = jnp.sum(got, axis=1)
        return carry

    lax.fori_loop(0, chunks * slabs, flux_body, 0)
    for step in slab_order:
        other, where = slab_peer(step)
        pltpu.make_async_remote_copy(
            src_ref=fl_send.at[other], dst_ref=fl_recv.at[step],
            send_sem=s_xs.at[step], recv_sem=s_xr.at[step], device_id=where, device_id_type=MESH,
        ).start()

    for h in range(strips):
        final(h)

    total = fl_send[me]
    for step in slab_order:
        other, where = slab_peer(step)
        pltpu.make_async_remote_copy(
            src_ref=fl_send.at[other], dst_ref=fl_recv.at[step],
            send_sem=s_xs.at[step], recv_sem=s_xr.at[step], device_id=where, device_id_type=MESH,
        ).wait()
        total = total + fl_recv[step]
    flux_out[...] = total


def shards(slabs, subs, groups, tables, images, bank, index, flux, noise, src_row, src_col):
    epochs, slab_rows, side = images.shape
    stamps, stamp, _ = bank.shape
    sources = src_row.shape[0]
    half = side // (2 * slabs)
    ext = half // strips + pad_rows
    width = side // groups
    per_dest = sources // slabs
    chunk = min(512, per_dest)
    f32 = jnp.float32
    vmem = pl.BlockSpec(memory_space=pltpu.VMEM)
    smem = pl.BlockSpec(memory_space=pltpu.SMEM)
    dma = pltpu.SemaphoreType.DMA
    plane = pltpu.VMEM((strips, slabs, epochs, 2 * half // strips, slab_rows), f32)
    return pl.pallas_call(
        functools.partial(kernel, slabs, subs, groups),
        out_shape=(
            jax.ShapeDtypeStruct((epochs, slab_rows, side), f32),
            jax.ShapeDtypeStruct((epochs, per_dest), f32),
        ),
        in_specs=[vmem, vmem, smem, smem, smem] + [vmem] * 8,
        out_specs=(vmem, vmem),
        scratch_shapes=[
            plane, plane, plane, plane,
            pltpu.VMEM((strips, epochs, 2, ext, side), f32),
            pltpu.VMEM((epochs * 2 * half, side), jnp.bfloat16),
            pltpu.VMEM((epochs * 2 * half, side), jnp.bfloat16),
            pltpu.VMEM((strips, stamps, 2, ext, side), f32),
            pltpu.VMEM((stamps, 8, 128), f32),
            pltpu.VMEM((8, 128), f32),
            pltpu.VMEM((groups, 8, 128), f32),
            pltpu.VMEM((strips, 2, ext, side), f32),
            pltpu.VMEM((strips, groups, 2, ext, width), f32),
            pltpu.VMEM((strips, groups, 2, ext, width), f32),
            pltpu.VMEM((strips, 2, ext, width), f32),
            pltpu.VMEM((strips, groups, 2, ext, width), f32),
            pltpu.VMEM((sources // chunk, side, chunk), jnp.bfloat16),
            pltpu.VMEM((sources // chunk, 2 * half, chunk), f32),
            pltpu.VMEM((slabs, epochs, per_dest), f32),
            pltpu.VMEM((slabs, epochs, per_dest), f32),
            dma((slabs, strips)), dma((slabs, strips)), dma((slabs, strips)), dma((slabs, strips)),
            dma((groups,)), dma((groups,)),
            dma((groups, strips)), dma((groups, strips)), dma((groups, strips)), dma((groups, strips)),
            dma((slabs,)), dma((slabs,)),
        ],
        compiler_params=pltpu.CompilerParams(
            collective_id=0, has_side_effects=True, vmem_limit_bytes=60 * 1024 * 1024
        ),
        name="zogy",
    )(images, bank, index, flux, noise, src_row.reshape(1, sources), src_col.reshape(1, sources), *tables)


def solution(mesh):
    subs = mesh.shape["sub"]
    slabs = mesh.shape["tile"] * subs
    groups = mesh.shape["epoch"]
    in_specs = (
        P(("grp", "epoch"), ("tile", "sub"), None),
        P(),
        P(("grp", "epoch")),
        P(("grp", "epoch")),
        P(("grp", "epoch")),
        P("grp"),
        P("grp"),
    )
    out_specs = (P(("grp", "epoch"), ("tile", "sub"), None), P(("grp", "epoch"), ("tile", "sub")))

    def run(images, bank, index, flux, noise, src_row, src_col):
        tables = make_tables(images.shape[2], slabs, bank.shape[1])
        body = functools.partial(shards, slabs, subs, groups, tables)
        return jax.shard_map(body, mesh=mesh, in_specs=in_specs, out_specs=out_specs, check_vma=False)(
            images, bank, index, flux, noise, src_row, src_col
        )

    return run
```
